32 devices in a mesh: dom: 16 (over z, x, core), sub: 2 (over y).
Axes of the slice: x: 2, y: 2, z: 4, core: 2. Of those that a mesh axis runs over, the one named last changes fastest.
Arguments:
- edge_vectors: float32 [3, 32768], P(None, ('dom', 'sub')), may hold values from -4.95 to 4.95, as said below
- senders: int32 [32768], P(('dom', 'sub')), may hold values from 0 to 175, as said below
- counts: int32 [1024], P(('dom', 'sub')), may hold values from 1 to 32, as said below
- species: int32 [1024], P(('dom', 'sub')), may hold values from 0 to 3
- send_list: int32 [512], P(('dom', 'sub')), may hold values from 0 to 31, as said below
- embed: float32 [128, 4], replicated, may hold values from -6 to 6
- radial_in1: float32 [64, 8], replicated, may hold values from -4 to 4
- radial_mid1: float32 [64, 64], replicated, may hold values from -1.5 to 1.5
- radial_out1: float32 [256, 64], replicated, may hold values from -1.5 to 1.5
- mix_s1: float32 [128, 128], replicated, may hold values from -0.5 to 0.5
- mix_v1: float32 [128, 128], replicated, may hold values from -0.5 to 0.5
- mix_q1: float32 [128, 128], replicated, may hold values from -0.25 to 0.25
- radial_in2: float32 [64, 8], replicated, may hold values from -4 to 4
- radial_mid2: float32 [64, 64], replicated, may hold values from -1.5 to 1.5
- radial_out2: float32 [512, 64], replicated, may hold values from -1.5 to 1.5
- mix_s2: float32 [128, 128], replicated, may hold values from -0.5 to 0.5
- mix_v2: float32 [128, 128], replicated, may hold values from -0.5 to 0.5
- mix_q2: float32 [128, 128], replicated, may hold values from -0.25 to 0.25
- read_lin: float32 [128], replicated, may hold values from -0.5 to 0.5
- read_hidden: float32 [16, 128], replicated, may hold values from -0.5 to 0.5
- read_out: float32 [16], replicated, may hold values from -1.5 to 1.5
Outputs:
- atom_energies: float32 [1024], P(('dom', 'sub'))
- forces: float32 [3, 1024], P(None, ('dom', 'sub'))
The draws below stay inside these ranges and needn't reach their ends.
Inputs may be any that keep to these rules, and one draw needn't show every extreme that they name: `senders`: A value t of 32 or more names entry (t - 32) % 16 of the send list of the device at offset (s // 3 - 1, s % 3 - 1) along (dom, sub), s = (t - 32) // 16; s is never 4 and never names a device outside the grid. `counts`: an atom's neighbours fill its first slots; the rest are padding. `send_list`: the 16 entries of one device are distinct atoms of that device, counted from its first atom. `edge_vectors`: every column has a length between 0.75 and 4.95.
All inputs are finite; a program needn't handle non-finite values.
Results may differ from the reference program's by a relative error of at most 0.000088.
Values sent between devices are 32-bit elements; how exact they have to be, the bound alone decides.
A program may use at most 64 MiB of HBM per device.

```python
import math
import jax
import jax.numpy as jnp
from jax import lax

C = 128
BASIS = 8
HID = 64
READ_HID = 16
SPECIES = 4
K = 32
ATOM_DEV = 32
GHOSTS = 16
ATOMS = 1024
EDGES = 32768
N_DOM = 16
N_SUB = 2


def draw_edge_vectors(key, part):
    dir_key, len_key = jax.random.split(key)
    direction = jax.random.normal(dir_key, (3, EDGES), jnp.float32)
    direction = direction / jnp.maximum(jnp.sqrt(jnp.sum(direction * direction, axis=0)), 0.001)[None, :]
    uniform = jax.random.uniform(len_key, (EDGES,), jnp.float32)
    length = 0.8 + 4.1 * uniform
    return direction * length[None, :]


def draw_senders(key, part):
    raw_key, spot_key = jax.random.split(jax.random.fold_in(key, 11))
    edge_ids = jnp.arange(EDGES, dtype=jnp.int32)
    device = edge_ids // (ATOM_DEV * K)
    domain = device // N_SUB
    subdom = device % N_SUB
    table_size = ATOM_DEV + 9 * GHOSTS
    raw = jax.random.randint(raw_key, (EDGES,), 0, table_size, dtype=jnp.int32)
    ghost_slot = jnp.maximum(raw - ATOM_DEV, 0) // GHOSTS
    near_dom = domain + ghost_slot // 3 - 1
    near_sub = subdom + ghost_slot % 3 - 1
    inside = (near_dom >= 0) & (near_dom < N_DOM) & (near_sub >= 0) & (near_sub < N_SUB)
    valid = (raw < ATOM_DEV) | (ghost_slot != 4) & inside
    chosen = jnp.where(valid, raw, raw % ATOM_DEV)
    spots = jax.random.randint(spot_key, (2,), 0, ATOM_DEV * K - 1, dtype=jnp.int32)
    chosen = chosen.at[spots[0]].set(table_size - 1)
    other_spot = (spots[0] + 1 + spots[1]) % (ATOM_DEV * K)
    chosen = chosen.at[other_spot].set(0)
    return chosen.astype(jnp.int32)


def draw_counts(key, part):
    cap_key, drop_key, spot_key = jax.random.split(jax.random.fold_in(key, 23), 3)
    devices = ATOMS // ATOM_DEV
    caps = jax.random.randint(cap_key, (devices,), K // 2, K + 1, dtype=jnp.int32)
    drops = jax.random.randint(drop_key, (ATOMS,), 0, K // 2, dtype=jnp.int32)
    filled = jnp.maximum(jnp.repeat(caps, ATOM_DEV) - drops, 1)
    spot = jax.random.randint(spot_key, (), 0, ATOMS, dtype=jnp.int32)
    return filled.at[spot].set(K).astype(jnp.int32)


def draw_send_list(key, part):
    devices = ATOMS // ATOM_DEV
    base_key = jax.random.fold_in(key, 37)

    def pick(index):
        return jax.random.permutation(jax.random.fold_in(base_key, index), ATOM_DEV)[:GHOSTS]
    return jax.vmap(pick)(jnp.arange(devices)).reshape(-1).astype(jnp.int32)


def place_ends(drawn, key, low, high):
    extent = drawn.shape
    spot = [jax.random.randint(jax.random.fold_in(key, axis), (), 0, extent[axis]) for axis in range(len(extent))]
    drawn = drawn.at[tuple(spot)].set(low)
    longest = extent.index(max(extent))
    spot[longest] = (spot[longest] + 1) % extent[longest]
    return drawn.at[tuple(spot)].set(high)


def gaussian(key, shape, scale, reach, held_as=jnp.bfloat16):
    values = jax.random.normal(key, shape, jnp.float32) * scale
    return jnp.minimum(jnp.maximum(values, -reach), reach).astype(held_as)


def setup_inputs(seed: int = 0) -> dict:
    arg_keys = jax.random.split(jax.random.key(seed), 22)
    return {
        "edge_vectors": draw_edge_vectors(jax.random.fold_in(arg_keys[21], 71), 0),
        "senders": draw_senders(jax.random.fold_in(arg_keys[21], 71), 0),
        "counts": draw_counts(jax.random.fold_in(arg_keys[21], 71), 0),
        "species": place_ends(jax.random.randint(arg_keys[3], (ATOMS,), 0, SPECIES), jax.random.fold_in(arg_keys[3], 1), 0, SPECIES - 1).astype(jnp.int32),
        "send_list": draw_send_list(jax.random.fold_in(arg_keys[21], 71), 0),
        "embed": gaussian(arg_keys[5], (C, SPECIES), 1.0, 6.0, jnp.float32),
        "radial_in1": gaussian(arg_keys[6], (HID, BASIS), (BASIS // 4) ** -0.5, 4.0, jnp.float32),
        "radial_mid1": gaussian(arg_keys[7], (HID, HID), (HID // 4) ** -0.5, 1.5, jnp.float32),
        "radial_out1": gaussian(arg_keys[8], (2 * C, HID), (HID // 4) ** -0.5, 1.5, jnp.float32),
        "mix_s1": gaussian(arg_keys[9], (C, C), C ** -0.5, 0.5, jnp.float32),
        "mix_v1": gaussian(arg_keys[10], (C, C), C ** -0.5, 0.5, jnp.float32),
        "mix_q1": gaussian(arg_keys[11], (C, C), (4 * C) ** -0.5, 0.25, jnp.float32),
        "radial_in2": gaussian(arg_keys[12], (HID, BASIS), (BASIS // 4) ** -0.5, 4.0, jnp.float32),
        "radial_mid2": gaussian(arg_keys[13], (HID, HID), (HID // 4) ** -0.5, 1.5, jnp.float32),
        "radial_out2": gaussian(arg_keys[14], (4 * C, HID), (HID // 4) ** -0.5, 1.5, jnp.float32),
        "mix_s2": gaussian(arg_keys[15], (C, C), C ** -0.5, 0.5, jnp.float32),
        "mix_v2": gaussian(arg_keys[16], (C, C), C ** -0.5, 0.5, jnp.float32),
        "mix_q2": gaussian(arg_keys[17], (C, C), (4 * C) ** -0.5, 0.25, jnp.float32),
        "read_lin": gaussian(arg_keys[18], (C,), C ** -0.5, 0.5, jnp.float32),
        "read_hidden": gaussian(arg_keys[19], (READ_HID, C), C ** -0.5, 0.5, jnp.float32),
        "read_out": gaussian(arg_keys[20], (READ_HID,), READ_HID ** -0.5, 1.5, jnp.float32),
    }


cutoff_radius = 5.0
exact = lax.Precision.HIGHEST

def radial_weights(distance, w_in, w_mid, w_out):
    scaled = distance / cutoff_radius
    envelope = 1.0 - 28.0 * scaled ** 6 + 48.0 * scaled ** 7 - 21.0 * scaled ** 8
    harmonic = jnp.arange(1, w_in.shape[1] + 1).astype(distance.dtype)[:, None]
    radial_basis = math.sqrt(2.0 / cutoff_radius) * jnp.sin(harmonic * (math.pi / cutoff_radius) * distance[None, :]) / distance[None, :] * envelope[None, :]
    hidden = jax.nn.silu(jnp.dot(w_in, radial_basis, precision=exact))
    hidden = jax.nn.silu(jnp.dot(w_mid, hidden, precision=exact))
    return jnp.dot(w_out, hidden, precision=exact)

def edge_messages(lookup, vectors, sources, live_mask, weights, slots):
    channels = lookup.shape[1]
    edges = vectors.shape[1]
    distance = jnp.sqrt(lax.optimization_barrier(jnp.sum(vectors * vectors, axis=0)))
    unit_dir = vectors / distance[None, :]
    radial = radial_weights(distance, weights[0], weights[1], weights[2]).reshape(-1, channels, edges) * live_mask[None, None, :]
    picked = jnp.take(lookup, sources, axis=2)
    scalar = picked[0]
    if lookup.shape[0] == 1:
        scalar_msg = radial[0] * scalar
        vector_msg = radial[1][None] * scalar[None] * unit_dir[:, None, :]
    else:
        vector = picked[1:]
        scalar_msg = radial[0] * scalar + radial[1] * lax.optimization_barrier(jnp.sum(unit_dir[:, None, :] * vector, axis=0))
        vector_msg = radial[2][None] * scalar[None] * unit_dir[:, None, :] + radial[3][None] * vector
    stacked = jnp.concatenate([scalar_msg[None], vector_msg], axis=0)
    return lax.optimization_barrier(jnp.sum(stacked.reshape(4, channels, edges // slots, slots), axis=3)) * slots ** (-0.5)

def node_update(aggregate, scalar, vector, mix_s, mix_v, mix_q):
    mixed_scalar = jnp.dot(mix_s, aggregate[0], precision=exact)
    mixed_vector = jnp.einsum('cd,kda->kca', mix_v, aggregate[1:], precision=exact)
    squares = mixed_scalar * mixed_scalar + lax.optimization_barrier(jnp.sum(mixed_vector * mixed_vector, axis=0))
    next_scalar = scalar + mixed_scalar + jnp.dot(mix_q, squares, precision=exact)
    next_vector = vector + mixed_vector + mixed_vector * mixed_scalar[None]
    return (next_scalar, next_vector)

def atom_energy(scalar_one, scalar_two, read_lin, read_hidden, read_out):
    second_term = jnp.dot(read_out, jax.nn.silu(jnp.dot(read_hidden, scalar_two, precision=exact)), precision=exact)
    return jnp.dot(read_lin, scalar_one, precision=exact) + second_term

def global_sources(senders, send_list):
    edge_ids = jnp.arange(EDGES).astype(jnp.int32)
    device = edge_ids // (ATOM_DEV * K)
    domain = device // N_SUB
    subdom = device % N_SUB
    offset = jnp.maximum(senders - ATOM_DEV, 0)
    ghost_slot = offset // GHOSTS
    list_entry = offset % GHOSTS
    near_dom = jnp.clip(domain + ghost_slot // 3 - 1, 0, N_DOM - 1)
    near_sub = jnp.clip(subdom + ghost_slot % 3 - 1, 0, N_SUB - 1)
    neighbour = near_dom * N_SUB + near_sub
    ghost_atom = neighbour * ATOM_DEV + send_list[(neighbour * GHOSTS + list_entry).astype(jnp.int32)]
    return jnp.where(senders < ATOM_DEV, device * ATOM_DEV + senders, ghost_atom).astype(jnp.int32)

def blockwise(lookup, vectors, sources, live_mask, weights):
    block_rows = math.gcd(ATOMS, 1024)
    block_count = ATOMS // block_rows
    vec_blocks = vectors.reshape(3, block_count, block_rows * K).transpose(1, 0, 2)

    def one_block(block_items):
        return edge_messages(lookup, block_items[0], block_items[1], block_items[2], weights, K)
    outputs = lax.map(jax.checkpoint(one_block), (vec_blocks, sources.reshape(block_count, -1), live_mask.reshape(block_count, -1)))
    return outputs.transpose(1, 2, 0, 3).reshape(4, -1, ATOMS)

def reference(edge_vectors, senders, counts, species, send_list, embed, radial_in1, radial_mid1, radial_out1, mix_s1, mix_v1, mix_q1, radial_in2, radial_mid2, radial_out2, mix_s2, mix_v2, mix_q2, read_lin, read_hidden, read_out):
    sources = global_sources(senders, send_list)
    live_mask = (jnp.arange(K)[None, :] < counts[:, None]).reshape(-1).astype(edge_vectors.dtype)
    species_hot = (jnp.arange(SPECIES)[:, None] == species[None, :]).astype(embed.dtype)
    initial = jnp.dot(embed, species_hot, precision=exact)
    layer_one = (radial_in1, radial_mid1, radial_out1)
    layer_two = (radial_in2, radial_mid2, radial_out2)

    def energies(vectors):
        agg_first = blockwise(initial[None], vectors, sources, live_mask, layer_one)
        scalar_one, vector_one = node_update(agg_first, initial, jnp.zeros((3,) + initial.shape, initial.dtype), mix_s1, mix_v1, mix_q1)
        lookup = jnp.concatenate([scalar_one[None], vector_one], axis=0)
        agg_second = blockwise(lookup, vectors, sources, live_mask, layer_two)
        scalar_two = node_update(agg_second, scalar_one, vector_one, mix_s2, mix_v2, mix_q2)[0]
        return atom_energy(scalar_one, scalar_two, read_lin, read_hidden, read_out)
    atom_energies, pullback = jax.vjp(energies, edge_vectors)
    edge_grads = pullback(jnp.ones_like(atom_energies))[0]
    received = lax.optimization_barrier(jnp.sum(edge_grads.reshape(3, ATOMS, K), axis=2))
    sent_part = jnp.zeros((3, ATOMS), edge_grads.dtype).at[:, sources].add(edge_grads)
    return (atom_energies, received - sent_part)
```

```python
import functools
import math

import jax
import jax.numpy as jnp
from jax import lax
from jax.experimental import pallas as pl
from jax.experimental.pallas import tpu as pltpu
from jax.sharding import PartitionSpec as P

cutoff_radius = 5.0
f32 = jnp.float32
bf16 = jnp.bfloat16
LANES = 128
MESH = pl.DeviceIdType.MESH


def mm(a, b, ca, cb):
    return lax.dot_general(a, b, (((ca,), (cb,)), ((), ())), preferred_element_type=f32)


def split(x):
    hi = x.astype(bf16)
    return hi, (x - hi.astype(f32)).astype(bf16)


def split3(x):
    hi = x.astype(bf16)
    rest = x - hi.astype(f32)
    mid = rest.astype(bf16)
    return hi, mid, (rest - mid.astype(f32)).astype(bf16)


def dot3(a, b, ca, cb):
    a_hi, a_lo = split(a)
    b_hi, b_lo = split(b)
    return mm(a_hi, b_hi, ca, cb) + (mm(a_hi, b_lo, ca, cb) + mm(a_lo, b_hi, ca, cb))


def hot2(hot, x, ca, cb):
    hi, lo = split(x)
    return mm(hot, hi, ca, cb) + mm(hot, lo, ca, cb)


def hot3(hot, x, ca, cb):
    hi, mid, lo = split3(x)
    return mm(hot, hi, ca, cb) + (mm(hot, mid, ca, cb) + mm(hot, lo, ca, cb))


def to_column(row):
    count = row.shape[1]
    shape = (count, count)
    same = lax.broadcasted_iota(jnp.int32, shape, 0) == lax.broadcasted_iota(jnp.int32, shape, 1)
    return jnp.sum(jnp.where(same, row, 0.0), axis=1, keepdims=True)


def series(t, first, terms):
    total = jnp.ones_like(t)
    for i in reversed(range(terms)):
        low = first + 2 * i
        total = 1.0 - t * (1.0 / (low * (low + 1))) * total
    return total


def kernel(
    n_dom,
    n_sub,
    vec_ref,
    senders_ref,
    counts_ref,
    species_ref,
    list_ref,
    embed_ref,
    win1_ref,
    wmid1_ref,
    wout1_ref,
    ms1_ref,
    mv1_ref,
    mq1_ref,
    win2_ref,
    wmid2_ref,
    wout2_ref,
    ms2_ref,
    mv2_ref,
    mq2_ref,
    lin_ref,
    rh_ref,
    ro_ref,
    energy_ref,
    force_ref,
    kinds,
    kinds_out,
    table,
    feat_out,
    grad_table,
    grad_in,
    force_table,
    force_in,
    live_hot,
    spec_hot,
    src_hot,
    v8,
    dbas,
    inv_ref,
    pack,
    rhs,
    winp,
    wmid,
    w1,
    w2,
    hid_ref,
    u_ref,
    ds1_ref,
    ds2_ref,
    rad_ref,
    x_ref,
    sums,
    agg2,
    dagg2,
    dh_ref,
    du_ref,
    gp_hi,
    gp_lo,
    qt,
    send_sem,
    recv_sem,
):
    dm, sb = lax.axis_index("dom"), lax.axis_index("sub")
    atoms = species_ref.shape[1]
    edges = vec_ref.shape[1]
    slots = edges // atoms
    ghosts = list_ref.shape[1]
    channels, kinds_n = embed_ref.shape
    hidden, n_basis = win1_ref.shape
    chunk = 8 * slots
    n_chunks = edges // chunk
    scale = slots ** (-0.5)
    C = channels
    sides = [s for s in range(9) if s != 4]

    def exists(s):
        ok = None
        for here, count, off in ((dm, n_dom, s // 3 - 1), (sb, n_sub, s % 3 - 1)):
            if off == 0:
                continue
            one = here > 0 if off < 0 else here < count - 1
            ok = one if ok is None else jnp.logical_and(ok, one)
        return ok

    def place(s):
        return (dm + (s // 3 - 1), sb + (s % 3 - 1))

    def copy_for(phase, s, src, dst, there):
        return pltpu.make_async_remote_copy(
            src_ref=src,
            dst_ref=dst,
            send_sem=send_sem.at[phase, s],
            recv_sem=recv_sem.at[phase, 8 - s],
            device_id=place(there),
            device_id_type=MESH,
        )

    def ghost_rows(s):
        return pl.ds(atoms + ghosts * s, ghosts)

    def copies(phase, s, there):
        pairs = (
            lambda k, r: (kinds_out, kinds.at[ghost_rows(r)]),
            lambda k, r: (feat_out, table.at[ghost_rows(r)]),
            lambda k, r: (grad_table.at[ghost_rows(k)], grad_in.at[r]),
            lambda k, r: (force_table.at[ghost_rows(k)], force_in.at[r]),
        )
        src, dst = pairs[phase](s, 8 - s)
        return copy_for(phase, s, src, dst, there)

    def send_all(phase):
        for s in sides:
            @pl.when(exists(s))
            def _():
                copies(phase, s, s).start()

    def wait_all(phase):
        for s in sides:
            @pl.when(exists(s))
            def _():
                copies(phase, s, s).wait_send()
                copies(phase, 8 - s, s).wait_recv()

    kinds[...] = jnp.zeros_like(kinds)
    table[...] = jnp.zeros_like(table)
    grad_in[...] = jnp.zeros_like(grad_in)
    force_in[...] = jnp.zeros_like(force_in)
    barrier = pltpu.get_barrier_semaphore()
    for s in sides:
        @pl.when(exists(s))
        def _():
            pl.semaphore_signal(barrier, inc=1, device_id=place(s), device_id_type=MESH)

    species_col = to_column(species_ref[...].astype(f32))
    counts_col = to_column(counts_ref[...].astype(f32)).astype(jnp.int32)
    list_col = to_column(list_ref[...].astype(f32))
    lane_a = lax.broadcasted_iota(jnp.int32, (atoms, LANES), 1).astype(f32)
    own_kinds = (species_col == lane_a).astype(f32)
    kinds[0:atoms, :] = own_kinds
    listed = (
        list_col == lax.broadcasted_iota(jnp.int32, (ghosts, atoms), 1).astype(f32)
    ).astype(f32).astype(bf16)
    kinds_out[...] = mm(listed, own_kinds.astype(bf16), 1, 0)
    near = [
        1 + jnp.where(at > 0, 1, 0) + jnp.where(at < count - 1, 1, 0)
        for at, count in ((dm, n_dom), (sb, n_sub))
    ]
    pl.semaphore_wait(barrier, near[0] * near[1] - 1)
    send_all(0)

    wmid[...] = jnp.zeros_like(wmid)
    wmid[0:hidden, 0:hidden] = wmid1_ref[...]
    wmid[hidden:, hidden:] = wmid2_ref[...]
    w1[...] = jnp.zeros_like(w1)
    w1[:, 0:hidden] = wout1_ref[...]
    w2[...] = jnp.zeros_like(w2)
    w2[:, hidden:] = wout2_ref[...]
    winp[...] = jnp.zeros_like(winp)
    winp[0:hidden, 0:n_basis] = win1_ref[...]
    winp[hidden:, 0:n_basis] = win2_ref[...]
    n_pack = 3 * n_basis
    row_i = lax.broadcasted_iota(jnp.int32, rhs.shape, 0)
    lane_i = lax.broadcasted_iota(jnp.int32, rhs.shape, 1)
    which = jnp.zeros(rhs.shape, f32)
    for k in range(3):
        in_rows = (row_i >= LANES * (k + 1)) & (row_i < LANES * (k + 2))
        for part in range(3):
            which = jnp.where(in_rows & (lane_i == n_pack + 8 * part + k), 1.0, which)
    rhs[...] = which
    for half, w_ref in enumerate((win1_ref, win2_ref)):
        hi, lo = split(w_ref[...])
        rows = slice(half * hidden, (half + 1) * hidden)
        rhs[rows, 0:n_basis] = hi.astype(f32)
        rhs[rows, n_basis : 2 * n_basis] = hi.astype(f32)
        rhs[rows, 2 * n_basis : 3 * n_basis] = lo.astype(f32)

    v8[...] = jnp.zeros_like(v8)
    v8[0:3, :] = vec_ref[...]
    vectors = v8[...]
    dist = jnp.sqrt(jnp.sum(vectors * vectors, axis=0, keepdims=True))
    inv = 1.0 / dist
    unit = vectors * inv
    v8[...] = unit
    inv_ref[...] = inv
    x1 = dist * (1.0 / cutoff_radius)
    x2 = x1 * x1
    x5 = x2 * x2 * x1
    x6 = x5 * x1
    env = 1.0 + x6 * (-28.0 + x1 * (48.0 - 21.0 * x1))
    denv = x5 * (-168.0 + x1 * (336.0 - 168.0 * x1)) * (1.0 / cutoff_radius)
    order = (lax.broadcasted_iota(jnp.int32, (n_basis, edges), 0) + 1).astype(f32)
    turns = order * x1
    near = jnp.floor(turns + 0.5)
    odd = near - 2.0 * jnp.floor(near * 0.5)
    sign = 1.0 - 2.0 * odd
    angle = (turns - near) * math.pi
    t = angle * angle
    sine = sign * angle * series(t, 2, 7)
    cosine = sign * series(t, 1, 7)
    norm = math.sqrt(2.0 / cutoff_radius)
    wave = (norm * inv) * sine
    basis = wave * env
    dbas[...] = ((norm * math.pi / cutoff_radius) * order * cosine * inv - wave * inv) * env + wave * denv

    b_hi, b_lo = split(basis)
    u_hi, u_mid, u_lo = split3(unit)
    parts = [b_hi, b_lo, b_hi, u_hi, u_mid, u_lo]
    pack[...] = jnp.concatenate([p.astype(f32) for p in parts], axis=0).astype(bf16)

    def rows_of(c):
        return pl.ds(pl.multiple_of(c * chunk, chunk), chunk)

    def radial_step(c, _):
        rows = rows_of(c)
        out = mm(pack[:, rows], rhs[...].astype(bf16), 0, 1)
        p1 = out[:, :LANES]
        u_ref[rows, :] = out[:, LANES:]
        s1 = jax.nn.sigmoid(p1)
        h1 = p1 * s1
        ds1_ref[rows, :] = s1 * (1.0 + p1 * (1.0 - s1))
        p2 = dot3(h1, wmid[...], 1, 1)
        s2 = jax.nn.sigmoid(p2)
        hid_ref[rows, :] = p2 * s2
        ds2_ref[rows, :] = s2 * (1.0 + p2 * (1.0 - s2))
        return 0

    lax.fori_loop(0, n_chunks, radial_step, 0)

    edge_i = lax.broadcasted_iota(jnp.int32, (atoms, edges), 1)
    atom_i = lax.broadcasted_iota(jnp.int32, (atoms, edges), 0)
    spot = edge_i - atom_i * slots
    live = ((spot >= 0) & (spot < counts_col)).astype(f32)
    live_hot[...] = live
    live_row = jnp.sum(live, axis=0, keepdims=True)
    entry_i = lax.broadcasted_iota(jnp.int32, src_hot.shape, 0)
    src_hot[...] = jnp.where(entry_i == senders_ref[...], live_row, 0.0).astype(bf16)

    own_kinds = kinds[0:atoms, :]
    spread_i = lax.broadcasted_iota(jnp.int32, (kinds_n * atoms, kinds_n), 0)
    kind_i = lax.broadcasted_iota(jnp.int32, (kinds_n * atoms, kinds_n), 1)
    spread = ((spread_i >= kind_i * atoms) & (spread_i < (kind_i + 1) * atoms)).astype(f32).astype(bf16)
    embed_rows = hot3(spread, embed_ref[...], 1, 1)
    initial = hot3(own_kinds[:, 0:kinds_n].astype(bf16), embed_ref[...], 1, 1)

    wait_all(0)
    seen = mm(kinds[...].astype(bf16), src_hot[...], 0, 0)
    for s in range(kinds_n):
        spec_hot[s * atoms : (s + 1) * atoms, :] = (live_hot[...] * seen[s : s + 1, :]).astype(bf16)

    sums[...] = jnp.zeros_like(sums)

    def first_step(c, _):
        rows = rows_of(c)
        hid = hid_ref[rows, :]
        hot = spec_hot[:, rows]
        sums[:, 0:LANES] += hot2(hot, hid, 1, 0)
        for k in range(3):
            lanes = slice(LANES * (k + 1), LANES * (k + 2))
            sums[:, lanes] += hot2(hot, hid * u_ref[rows, LANES * k : LANES * (k + 1)], 1, 0)
        return 0

    lax.fori_loop(0, n_chunks, first_step, 0)

    def by_kind(x):
        total = x[0:atoms]
        for s in range(1, kinds_n):
            total = total + x[s * atoms : (s + 1) * atoms]
        return total

    agg = []
    for k in range(4):
        weight = w1[0:C, :] if k == 0 else w1[C : 2 * C, :]
        spread_agg = dot3(sums[:, LANES * k : LANES * (k + 1)], weight, 1, 1)
        agg.append(by_kind(spread_agg * embed_rows) * scale)

    def mixed(parts, ms, mv, mq):
        a = dot3(parts[0], ms, 1, 1)
        b = dot3(jnp.concatenate(parts[1:], axis=0), mv, 1, 1)
        b = [b[k * atoms : (k + 1) * atoms] for k in range(3)]
        squares = a * a + (b[0] * b[0] + b[1] * b[1] + b[2] * b[2])
        return a, b, dot3(squares, mq, 1, 1)

    a1, b1, q1 = mixed(agg, ms1_ref[...], mv1_ref[...], mq1_ref[...])
    scalar_one = initial + a1 + q1
    feats = [scalar_one] + [b + b * a1 for b in b1]
    for k in range(4):
        table[0:atoms, C * k : C * (k + 1)] = feats[k]
        feat_out[:, C * k : C * (k + 1)] = hot3(listed, feats[k], 1, 0)
    send_all(1)

    def second_radial(c, _):
        rows = rows_of(c)
        rad_ref[rows, :] = dot3(hid_ref[rows, :], w2[...], 1, 1)
        return 0

    lax.fori_loop(0, n_chunks, second_radial, 0)
    wait_all(1)

    def second_step(c, _):
        rows = rows_of(c)
        x = hot2(src_hot[:, rows], table[...], 0, 0)
        x_ref[rows, :] = x
        s, v = x[:, :C], [x[:, C * k : C * (k + 1)] for k in (1, 2, 3)]
        u = [u_ref[rows, LANES * k : LANES * (k + 1)] for k in range(3)]
        r = [rad_ref[rows, C * k : C * (k + 1)] for k in range(4)]
        uv = u[0] * v[0] + u[1] * v[1] + u[2] * v[2]
        rs = r[2] * s
        msgs = [r[0] * s + r[1] * uv] + [rs * u[k] + r[3] * v[k] for k in range(3)]
        group = pl.ds(pl.multiple_of(c * 8, 8), 8)
        for k in range(4):
            agg2[group, C * k : C * (k + 1)] = jnp.sum(msgs[k].reshape(8, slots, C), axis=1) * scale
        return 0

    lax.fori_loop(0, n_chunks, second_step, 0)

    parts = [agg2[:, C * k : C * (k + 1)] for k in range(4)]
    a2, b2, q2 = mixed(parts, ms2_ref[...], mv2_ref[...], mq2_ref[...])
    scalar_two = scalar_one + a2 + q2
    z = dot3(scalar_two, rh_ref[...], 1, 1)
    sz = jax.nn.sigmoid(z)
    lin8 = jnp.broadcast_to(lin_ref[...], (8, C))
    ro8 = jnp.broadcast_to(ro_ref[...], (8, ro_ref.shape[1]))
    energy = dot3(lin8, scalar_one, 1, 1) + dot3(ro8, z * sz, 1, 1)
    energy_ref[...] = energy[0:1, :]

    dz = ro_ref[...] * (sz * (1.0 + z * (1.0 - sz)))
    ds_two = dot3(dz, rh_ref[...], 1, 0)
    dq = dot3(ds_two, mq2_ref[...], 1, 0)
    da = ds_two + 2.0 * a2 * dq
    dagg2[:, 0:C] = dot3(da, ms2_ref[...], 1, 0) * scale
    db = dot3(jnp.concatenate([2.0 * b * dq for b in b2], axis=0), mv2_ref[...], 1, 0) * scale
    for k in range(3):
        dagg2[:, C * (k + 1) : C * (k + 2)] = db[k * atoms : (k + 1) * atoms]
    ds_direct = ds_two + lin_ref[...]

    def pick_lane(k, rows_n):
        lane = lax.broadcasted_iota(jnp.int32, (rows_n, LANES), 1)
        return (lane == 8 + k).astype(f32).astype(bf16)

    grad_table[...] = jnp.zeros_like(grad_table)

    def second_back(c, _):
        rows = rows_of(c)
        group = pl.ds(pl.multiple_of(c * 8, 8), 8)
        d = []
        for k in range(4):
            small = dagg2[group, C * k : C * (k + 1)]
            d.append(jnp.broadcast_to(small[:, None, :], (8, slots, C)).reshape(chunk, C))
        s, v = x_ref[rows, 0:C], [x_ref[rows, C * k : C * (k + 1)] for k in (1, 2, 3)]
        u = [u_ref[rows, LANES * k : LANES * (k + 1)] for k in range(3)]
        r = [rad_ref[rows, C * k : C * (k + 1)] for k in range(4)]
        uv = u[0] * v[0] + u[1] * v[1] + u[2] * v[2]
        ud = u[0] * d[1] + u[1] * d[2] + u[2] * d[3]
        dv = d[1] * v[0] + d[2] * v[1] + d[3] * v[2]
        drad = jnp.concatenate([d[0] * s, d[0] * uv, s * ud, dv], axis=1)
        dh_ref[rows, :] = dot3(drad, w2[...], 1, 0)
        hot = src_hot[:, rows]
        r1d = r[1] * d[0]
        r2s = r[2] * s
        grad_table[:, 0:C] += hot2(hot, r[0] * d[0] + r[2] * ud, 1, 0)
        du = jnp.zeros((chunk, LANES), f32)
        for k in range(3):
            lanes = slice(C * (k + 1), C * (k + 2))
            grad_table[:, lanes] += hot2(hot, r1d * u[k] + r[3] * d[k + 1], 1, 0)
            hi, lo = split(r1d * v[k] + r2s * d[k + 1])
            pick = pick_lane(k, C)
            du = du + (mm(hi, pick, 1, 0) + mm(lo, pick, 1, 0))
        du_ref[rows, :] = du
        return 0

    lax.fori_loop(0, n_chunks, second_back, 0)
    send_all(2)
    wait_all(2)
    ghost_grad = grad_in[0]
    for s in range(1, 9):
        ghost_grad = ghost_grad + grad_in[s]
    dfeat = grad_table[0:atoms, :] + hot3(listed, ghost_grad, 0, 0)
    ds = dfeat[:, 0:C] + ds_direct
    dv = [dfeat[:, C * k : C * (k + 1)] for k in (1, 2, 3)]
    dq = dot3(ds, mq1_ref[...], 1, 0)
    da = ds + 2.0 * a1 * dq + (dv[0] * b1[0] + dv[1] * b1[1] + dv[2] * b1[2])
    db = [dv[k] * (1.0 + a1) + 2.0 * b1[k] * dq for k in range(3)]
    dagg = [dot3(da, ms1_ref[...], 1, 0) * scale]
    db = dot3(jnp.concatenate(db, axis=0), mv1_ref[...], 1, 0) * scale
    dagg += [db[k * atoms : (k + 1) * atoms] for k in range(3)]
    for k in range(4):
        weight = w1[0:C, :] if k == 0 else w1[C : 2 * C, :]
        spread_grad = jnp.concatenate([dagg[k]] * kinds_n, axis=0) * embed_rows
        hi, lo = split(dot3(spread_grad, weight, 1, 0))
        gp_hi[:, LANES * k : LANES * (k + 1)] = hi
        gp_lo[:, LANES * k : LANES * (k + 1)] = lo

    def first_back(c, _):
        rows = rows_of(c)
        hot = spec_hot[:, rows]
        g = mm(hot, gp_hi[...], 0, 0) + mm(hot, gp_lo[...], 0, 0)
        hid = hid_ref[rows, :]
        dh = dh_ref[rows, :] + g[:, 0:LANES]
        q = du_ref[rows, :]
        for k in range(3):
            gk = g[:, LANES * (k + 1) : LANES * (k + 2)]
            dh = dh + u_ref[rows, LANES * k : LANES * (k + 1)] * gk
            hi, lo = split(hid * gk)
            pick = pick_lane(k, LANES)
            q = q + (mm(hi, pick, 1, 0) + mm(lo, pick, 1, 0))
        dp2 = dh * ds2_ref[rows, :]
        dp1 = dot3(dp2, wmid[...], 1, 0) * ds1_ref[rows, :]
        q = q + dot3(dp1, winp[...], 1, 0)
        qt[:, rows] = jnp.transpose(q)
        return 0

    lax.fori_loop(0, n_chunks, first_back, 0)

    unit = v8[...]
    inv = inv_ref[...]
    dr = jnp.sum(qt[0:n_basis, :] * dbas[...], axis=0, keepdims=True)
    du = qt[8:16, :]
    along = jnp.sum(unit * du, axis=0, keepdims=True)
    g8 = dr * unit + (du - unit * along) * inv
    g_hi, g_mid, g_lo = split3(g8)
    hot = src_hot[...]
    force_table[...] = jnp.zeros_like(force_table)
    force_table[:, 0:8] = mm(hot, g_hi, 1, 1) + (mm(hot, g_mid, 1, 1) + mm(hot, g_lo, 1, 1))
    send_all(3)
    own = (live_hot[...] - src_hot[0:atoms, :].astype(f32)).astype(bf16)
    force = mm(g_hi, own, 1, 1) + (mm(g_mid, own, 1, 1) + mm(g_lo, own, 1, 1))
    wait_all(3)
    ghost_force = force_in[0]
    for s in range(1, 9):
        ghost_force = ghost_force + force_in[s]
    hi, mid, lo = split3(ghost_force)
    late = mm(hi, listed, 0, 0) + (mm(mid, listed, 0, 0) + mm(lo, listed, 0, 0))
    force_ref[...] = (force - late[0:8, :])[0:3, :]


def on_device(n_dom, n_sub, *args):
    (vec, senders, counts, species, send_list, embed) = args[:6]
    weights = list(args[6:18])
    read_lin, read_hidden, read_out = args[18:]
    edges = vec.shape[1]
    atoms = species.shape[0]
    ghosts = send_list.shape[0]
    channels, kinds_n = embed.shape
    hidden, n_basis = weights[0].shape
    entries = -(-(atoms + 9 * ghosts) // LANES) * LANES
    wide = 4 * channels
    row = lambda x: x.reshape(1, -1)
    scratch = [
        ((entries, LANES), f32),
        ((ghosts, LANES), f32),
        ((entries, wide), f32),
        ((ghosts, wide), f32),
        ((entries, wide), f32),
        ((9, ghosts, wide), f32),
        ((entries, LANES), f32),
        ((9, ghosts, LANES), f32),
        ((atoms, edges), f32),
        ((kinds_n * atoms, edges), bf16),
        ((entries, edges), bf16),
        ((8, edges), f32),
        ((n_basis, edges), f32),
        ((1, edges), f32),
        ((3 * n_basis + 24, edges), bf16),
        ((4 * LANES, 3 * n_basis + 24), f32),
        ((LANES, LANES), f32),
        ((LANES, LANES), f32),
        ((2 * channels, LANES), f32),
        ((4 * channels, LANES), f32),
        ((edges, LANES), f32),
        ((edges, 3 * LANES), f32),
        ((edges, LANES), f32),
        ((edges, LANES), f32),
        ((edges, wide), f32),
        ((edges, wide), f32),
        ((kinds_n * atoms, 4 * LANES), f32),
        ((atoms, wide), f32),
        ((atoms, wide), f32),
        ((edges, LANES), f32),
        ((edges, LANES), f32),
        ((kinds_n * atoms, 4 * LANES), bf16),
        ((kinds_n * atoms, 4 * LANES), bf16),
        ((LANES, edges), f32),
    ]
    whole = pl.BlockSpec(memory_space=pltpu.VMEM)
    energy, force = pl.pallas_call(
        functools.partial(kernel, n_dom, n_sub),
        out_shape=(
            jax.ShapeDtypeStruct((1, atoms), f32),
            jax.ShapeDtypeStruct((3, atoms), f32),
        ),
        in_specs=[whole] * 21,
        out_specs=(whole, whole),
        scratch_shapes=[pltpu.VMEM(shape, dtype) for shape, dtype in scratch]
        + [pltpu.SemaphoreType.DMA((4, 9)), pltpu.SemaphoreType.DMA((4, 9))],
        compiler_params=pltpu.CompilerParams(
            collective_id=0, has_side_effects=True, vmem_limit_bytes=56 * 1024 * 1024
        ),
    )(
        vec,
        row(senders),
        row(counts),
        row(species),
        row(send_list),
        embed,
        *weights,
        row(read_lin),
        read_hidden,
        row(read_out),
    )
    return energy.reshape(-1), force


def solution(mesh):
    one = P(("dom", "sub"))
    return jax.shard_map(
        functools.partial(on_device, mesh.shape["dom"], mesh.shape["sub"]),
        mesh=mesh,
        in_specs=(P(None, ("dom", "sub")), one, one, one, one) + (P(),) * 16,
        out_specs=(one, P(None, ("dom", "sub"))),
        check_vma=False,
    )
```

```python
import functools
import math

import jax
import jax.numpy as jnp
from jax import lax
from jax.experimental import pallas as pl
from jax.experimental.pallas import tpu as pltpu
from jax.sharding import PartitionSpec as P

cutoff_radius = 5.0
f32 = jnp.float32
bf16 = jnp.bfloat16
LANES = 128
MESH = pl.DeviceIdType.MESH


def mm(a, b, ca, cb):
    return lax.dot_general(a, b, (((ca,), (cb,)), ((), ())), preferred_element_type=f32)


def split(x):
    hi = x.astype(bf16)
    return hi, (x - hi.astype(f32)).astype(bf16)


def split3(x):
    hi = x.astype(bf16)
    rest = x - hi.astype(f32)
    mid = rest.astype(bf16)
    return hi, mid, (rest - mid.astype(f32)).astype(bf16)


def dot3(a, b, ca, cb):
    a_hi, a_lo = split(a)
    b_hi, b_lo = split(b)
    return mm(a_hi, b_hi, ca, cb) + (mm(a_hi, b_lo, ca, cb) + mm(a_lo, b_hi, ca, cb))


def hot2(hot, x, ca, cb):
    hi, lo = split(x)
    return mm(hot, hi, ca, cb) + mm(hot, lo, ca, cb)


def hot3(hot, x, ca, cb):
    hi, mid, lo = split3(x)
    return mm(hot, hi, ca, cb) + (mm(hot, mid, ca, cb) + mm(hot, lo, ca, cb))


def to_column(row):
    count = row.shape[1]
    shape = (count, count)
    same = lax.broadcasted_iota(jnp.int32, shape, 0) == lax.broadcasted_iota(jnp.int32, shape, 1)
    return jnp.sum(jnp.where(same, row, 0.0), axis=1, keepdims=True)


def series(t, first, terms):
    total = jnp.ones_like(t)
    for i in reversed(range(terms)):
        low = first + 2 * i
        total = 1.0 - t * (1.0 / (low * (low + 1))) * total
    return total


def kernel(
    n_dom,
    n_sub,
    vec_ref,
    senders_ref,
    counts_ref,
    species_ref,
    list_ref,
    embed_ref,
    win1_ref,
    wmid1_ref,
    wout1_ref,
    ms1_ref,
    mv1_ref,
    mq1_ref,
    win2_ref,
    wmid2_ref,
    wout2_ref,
    ms2_ref,
    mv2_ref,
    mq2_ref,
    lin_ref,
    rh_ref,
    ro_ref,
    energy_ref,
    force_ref,
    kinds,
    kinds_out,
    table,
    feat_out,
    grad_table,
    grad_in,
    force_table,
    force_in,
    live_hot,
    spec_hot,
    src_hot,
    v8,
    dbas,
    inv_ref,
    pack,
    rhs,
    wide_rhs,
    winp,
    winp_k,
    wmid,
    wmid_f,
    wmid_b,
    w1,
    w2_k,
    hid_ref,
    u_ref,
    ds1_ref,
    ds2_ref,
    rad_ref,
    x_ref,
    sums,
    agg2,
    dagg2,
    dh_ref,
    du_ref,
    gp,
    qt,
    send_sem,
    recv_sem,
):
    dm, sb = lax.axis_index("dom"), lax.axis_index("sub")
    atoms = species_ref.shape[1]
    edges = vec_ref.shape[1]
    slots = edges // atoms
    ghosts = list_ref.shape[1]
    kinds_n, channels = embed_ref.shape
    n_basis, hidden = win1_ref.shape
    chunk = 8 * slots
    n_chunks = edges // chunk
    scale = slots ** (-0.5)
    C = channels
    sides = [s for s in range(9) if s != 4]

    def exists(s):
        ok = None
        for here, count, off in ((dm, n_dom, s // 3 - 1), (sb, n_sub, s % 3 - 1)):
            if off == 0:
                continue
            one = here > 0 if off < 0 else here < count - 1
            ok = one if ok is None else jnp.logical_and(ok, one)
        return ok

    def place(s):
        return (dm + (s // 3 - 1), sb + (s % 3 - 1))

    def copy_for(phase, s, src, dst, there):
        return pltpu.make_async_remote_copy(
            src_ref=src,
            dst_ref=dst,
            send_sem=send_sem.at[phase, s],
            recv_sem=recv_sem.at[phase, 8 - s],
            device_id=place(there),
            device_id_type=MESH,
        )

    def ghost_rows(s):
        return pl.ds(atoms + ghosts * s, ghosts)

    def copies(phase, s, there):
        pairs = (
            lambda k, r: (kinds_out, kinds.at[ghost_rows(r)]),
            lambda k, r: (feat_out, table.at[ghost_rows(r)]),
            lambda k, r: (grad_table.at[ghost_rows(k)], grad_in.at[r]),
            lambda k, r: (force_table.at[ghost_rows(k)], force_in.at[r]),
        )
        src, dst = pairs[phase](s, 8 - s)
        return copy_for(phase, s, src, dst, there)

    def send_all(phase):
        for s in sides:
            @pl.when(exists(s))
            def _():
                copies(phase, s, s).start()

    def wait_all(phase):
        for s in sides:
            @pl.when(exists(s))
            def _():
                copies(phase, s, s).wait_send()
                copies(phase, 8 - s, s).wait_recv()

    kinds[...] = jnp.zeros_like(kinds)
    table[...] = jnp.zeros_like(table)
    grad_in[...] = jnp.zeros_like(grad_in)
    force_in[...] = jnp.zeros_like(force_in)
    barrier = pltpu.get_barrier_semaphore()
    for s in sides:
        @pl.when(exists(s))
        def _():
            pl.semaphore_signal(barrier, inc=1, device_id=place(s), device_id_type=MESH)

    species_col = to_column(species_ref[...].astype(f32))
    counts_col = to_column(counts_ref[...].astype(f32)).astype(jnp.int32)
    list_col = to_column(list_ref[...].astype(f32))
    lane_a = lax.broadcasted_iota(jnp.int32, (atoms, LANES), 1).astype(f32)
    own_kinds = (species_col == lane_a).astype(f32)
    kinds[0:atoms, :] = own_kinds
    listed = (
        list_col == lax.broadcasted_iota(jnp.int32, (ghosts, atoms), 1).astype(f32)
    ).astype(f32).astype(bf16)
    kinds_out[...] = mm(listed, own_kinds.astype(bf16), 1, 0)
    near = [
        1 + jnp.where(at > 0, 1, 0) + jnp.where(at < count - 1, 1, 0)
        for at, count in ((dm, n_dom), (sb, n_sub))
    ]
    pl.semaphore_wait(barrier, near[0] * near[1] - 1)
    send_all(0)

    wmid[...] = jnp.zeros_like(wmid)
    wmid[0:hidden, 0:hidden] = wmid1_ref[...]
    wmid[hidden:, hidden:] = wmid2_ref[...]
    hi, lo = split(wmid[...])
    wmid_f[...] = jnp.concatenate([hi, hi, lo], axis=1)
    wmid_b[...] = jnp.concatenate([hi, hi, lo], axis=0)
    w1[...] = jnp.zeros_like(w1)
    w1[0:hidden, :] = wout1_ref[...]
    hi, lo = split(wout2_ref[...])
    w2_k[...] = jnp.concatenate([lo, hi, jnp.zeros_like(hi), hi], axis=0)
    winp[...] = jnp.zeros_like(winp)
    winp[0:n_basis, 0:hidden] = win1_ref[...]
    winp[0:n_basis, hidden:] = win2_ref[...]
    hi, lo = split(winp[...])
    winp_k[...] = jnp.concatenate([hi, hi, lo], axis=1)
    n_pack = 3 * n_basis
    row_i = lax.broadcasted_iota(jnp.int32, rhs.shape, 0)
    lane_i = lax.broadcasted_iota(jnp.int32, rhs.shape, 1)
    which = jnp.zeros(rhs.shape, f32)
    for k in range(3):
        in_lanes = (lane_i >= LANES * (k + 1)) & (lane_i < LANES * (k + 2))
        for part in range(3):
            which = jnp.where(in_lanes & (row_i == n_pack + 8 * part + k), 1.0, which)
    rhs[...] = which
    hi, lo = split(winp[0:n_basis, :])
    rhs[0:n_basis, 0:LANES] = hi.astype(f32)
    rhs[n_basis : 2 * n_basis, 0:LANES] = hi.astype(f32)
    rhs[2 * n_basis : 3 * n_basis, 0:LANES] = lo.astype(f32)
    wide_rhs[...] = rhs[...].astype(bf16)

    def dot_k(a, stacked, dim):
        a_hi, a_lo = split(a)
        both = jnp.concatenate([a_hi, a_lo], axis=1)
        if dim == 1:
            first, last = stacked[:, : 2 * LANES], stacked[:, 2 * LANES :]
        else:
            first, last = stacked[: 2 * LANES, :], stacked[2 * LANES :, :]
        return mm(both, first, 1, dim) + mm(a_hi, last, 1, dim)

    def upper_half(x, other):
        lane = lax.broadcasted_iota(jnp.int32, x.shape, 1)
        return jnp.where(lane >= hidden, x, other)

    v8[...] = jnp.zeros_like(v8)
    v8[0:3, :] = vec_ref[...]
    vectors = v8[...]
    dist = jnp.sqrt(jnp.sum(vectors * vectors, axis=0, keepdims=True))
    inv = 1.0 / dist
    unit = vectors * inv
    v8[...] = unit
    inv_ref[...] = inv
    x1 = dist * (1.0 / cutoff_radius)
    x2 = x1 * x1
    x5 = x2 * x2 * x1
    x6 = x5 * x1
    env = 1.0 + x6 * (-28.0 + x1 * (48.0 - 21.0 * x1))
    denv = x5 * (-168.0 + x1 * (336.0 - 168.0 * x1)) * (1.0 / cutoff_radius)
    order = (lax.broadcasted_iota(jnp.int32, (n_basis, edges), 0) + 1).astype(f32)
    turns = order * x1
    near = jnp.floor(turns + 0.5)
    odd = near - 2.0 * jnp.floor(near * 0.5)
    sign = 1.0 - 2.0 * odd
    angle = (turns - near) * math.pi
    t = angle * angle
    sine = sign * angle * series(t, 2, 7)
    cosine = sign * series(t, 1, 7)
    norm = math.sqrt(2.0 / cutoff_radius)
    wave = (norm * inv) * sine
    basis = wave * env
    dbas[...] = ((norm * math.pi / cutoff_radius) * order * cosine * inv - wave * inv) * env + wave * denv

    b_hi, b_lo = split(basis)
    u_hi, u_mid, u_lo = split3(unit)
    parts = [b_hi, b_lo, b_hi, u_hi, u_mid, u_lo]
    pack[...] = jnp.concatenate([p.astype(f32) for p in parts], axis=0).astype(bf16)

    def rows_of(c):
        return pl.ds(pl.multiple_of(c * chunk, chunk), chunk)

    def radial_step(c, _):
        rows = rows_of(c)
        out = mm(pack[:, rows], wide_rhs[...], 0, 0)
        p1 = out[:, :LANES]
        u_ref[rows, :] = out[:, LANES:]
        s1 = jax.nn.sigmoid(p1)
        h1 = p1 * s1
        ds1_ref[rows, :] = s1 * (1.0 + p1 * (1.0 - s1))
        p2 = dot_k(h1, wmid_f, 1)
        s2 = jax.nn.sigmoid(p2)
        hid_ref[rows, :] = p2 * s2
        ds2_ref[rows, :] = s2 * (1.0 + p2 * (1.0 - s2))
        return 0

    lax.fori_loop(0, n_chunks, radial_step, 0)

    edge_i = lax.broadcasted_iota(jnp.int32, (atoms, edges), 1)
    atom_i = lax.broadcasted_iota(jnp.int32, (atoms, edges), 0)
    spot = edge_i - atom_i * slots
    live = ((spot >= 0) & (spot < counts_col)).astype(f32)
    live_hot[...] = live
    live_row = jnp.sum(live, axis=0, keepdims=True)
    entry_i = lax.broadcasted_iota(jnp.int32, src_hot.shape, 0)
    src_hot[...] = jnp.where(entry_i == senders_ref[...], live_row, 0.0).astype(bf16)

    own_kinds = kinds[0:atoms, :]
    spread_i = lax.broadcasted_iota(jnp.int32, (kinds_n * atoms, kinds_n), 0)
    kind_i = lax.broadcasted_iota(jnp.int32, (kinds_n * atoms, kinds_n), 1)
    spread = ((spread_i >= kind_i * atoms) & (spread_i < (kind_i + 1) * atoms)).astype(f32).astype(bf16)
    embed_rows = hot3(spread, embed_ref[...], 1, 0)
    initial = hot3(own_kinds[:, 0:kinds_n].astype(bf16), embed_ref[...], 1, 0)

    wait_all(0)
    seen = mm(kinds[...].astype(bf16), src_hot[...], 0, 0)
    for s in range(kinds_n):
        hot = (live_hot[...] * seen[s : s + 1, :]).astype(bf16)
        spec_hot[s * atoms : (s + 1) * atoms, :] = hot
        spec_hot[(kinds_n + s) * atoms : (kinds_n + s + 1) * atoms, :] = hot

    sums[...] = jnp.zeros_like(sums)

    def first_step(c, _):
        rows = rows_of(c)
        hid = hid_ref[rows, :]
        hot = spec_hot[0 : kinds_n * atoms, rows]
        turned = [hid * u_ref[rows, LANES * k : LANES * (k + 1)] for k in range(3)]
        sums[...] += hot2(hot, jnp.concatenate([hid] + turned, axis=1), 1, 0)
        return 0

    lax.fori_loop(0, n_chunks, first_step, 0)

    def by_kind(x):
        total = x[0:atoms]
        for s in range(1, kinds_n):
            total = total + x[s * atoms : (s + 1) * atoms]
        return total

    agg = []
    for k in range(4):
        weight = w1[:, 0:C] if k == 0 else w1[:, C : 2 * C]
        spread_agg = dot3(sums[:, LANES * k : LANES * (k + 1)], weight, 1, 0)
        agg.append(by_kind(spread_agg * embed_rows) * scale)

    def mixed(parts, ms, mv, mq):
        a = dot3(parts[0], ms, 1, 1)
        b = dot3(jnp.concatenate(parts[1:], axis=0), mv, 1, 1)
        b = [b[k * atoms : (k + 1) * atoms] for k in range(3)]
        squares = a * a + (b[0] * b[0] + b[1] * b[1] + b[2] * b[2])
        return a, b, dot3(squares, mq, 1, 1)

    a1, b1, q1 = mixed(agg, ms1_ref[...], mv1_ref[...], mq1_ref[...])
    scalar_one = initial + a1 + q1
    feats = [scalar_one] + [b + b * a1 for b in b1]
    for k in range(4):
        table[0:atoms, C * k : C * (k + 1)] = feats[k]
        feat_out[:, C * k : C * (k + 1)] = hot3(listed, feats[k], 1, 0)
    send_all(1)

    def second_radial(c, _):
        rows = rows_of(c)
        hid = hid_ref[rows, :]
        twice = upper_half(hid, pltpu.roll(hid, hidden, 1)).astype(bf16)
        rest = split(hid)[1]
        rad_ref[rows, :] = mm(jnp.concatenate([twice, rest], axis=1), w2_k[...], 1, 0)
        return 0

    lax.fori_loop(0, n_chunks, second_radial, 0)
    wait_all(1)

    def second_step(c, _):
        rows = rows_of(c)
        x = hot2(src_hot[:, rows], table[...], 0, 0)
        x_ref[rows, :] = x
        s, v = x[:, :C], [x[:, C * k : C * (k + 1)] for k in (1, 2, 3)]
        u = [u_ref[rows, LANES * k : LANES * (k + 1)] for k in range(3)]
        r = [rad_ref[rows, C * k : C * (k + 1)] for k in range(4)]
        uv = u[0] * v[0] + u[1] * v[1] + u[2] * v[2]
        rs = r[2] * s
        msgs = [r[0] * s + r[1] * uv] + [rs * u[k] + r[3] * v[k] for k in range(3)]
        group = pl.ds(pl.multiple_of(c * 8, 8), 8)
        for k in range(4):
            agg2[group, C * k : C * (k + 1)] = jnp.sum(msgs[k].reshape(8, slots, C), axis=1) * scale
        return 0

    lax.fori_loop(0, n_chunks, second_step, 0)

    parts = [agg2[:, C * k : C * (k + 1)] for k in range(4)]
    a2, b2, q2 = mixed(parts, ms2_ref[...], mv2_ref[...], mq2_ref[...])
    scalar_two = scalar_one + a2 + q2
    z = dot3(scalar_two, rh_ref[...], 1, 1)
    sz = jax.nn.sigmoid(z)
    lin8 = jnp.broadcast_to(lin_ref[...], (8, C))
    ro8 = jnp.broadcast_to(ro_ref[...], (8, ro_ref.shape[1]))
    energy = dot3(lin8, scalar_one, 1, 1) + dot3(ro8, z * sz, 1, 1)
    energy_ref[...] = energy[0:1, :]

    dz = ro_ref[...] * (sz * (1.0 + z * (1.0 - sz)))
    ds_two = dot3(dz, rh_ref[...], 1, 0)
    dq = dot3(ds_two, mq2_ref[...], 1, 0)
    da = ds_two + 2.0 * a2 * dq
    dagg2[:, 0:C] = dot3(da, ms2_ref[...], 1, 0) * scale
    db = dot3(jnp.concatenate([2.0 * b * dq for b in b2], axis=0), mv2_ref[...], 1, 0) * scale
    for k in range(3):
        dagg2[:, C * (k + 1) : C * (k + 2)] = db[k * atoms : (k + 1) * atoms]
    ds_direct = ds_two + lin_ref[...]

    def lane_sum(k, x):
        lane = lax.broadcasted_iota(jnp.int32, x.shape, 1)
        return jnp.where(lane == 8 + k, jnp.sum(x, axis=1, keepdims=True), 0.0)

    grad_table[...] = jnp.zeros_like(grad_table)

    def spread_rows(c):
        group = pl.ds(pl.multiple_of(c * 8, 8), 8)
        out = []
        for k in range(4):
            small = dagg2[group, C * k : C * (k + 1)]
            out.append(jnp.broadcast_to(small[:, None, :], (8, slots, C)).reshape(chunk, C))
        return out

    def second_scatter(c, _):
        rows = rows_of(c)
        d = spread_rows(c)
        u = [u_ref[rows, LANES * k : LANES * (k + 1)] for k in range(3)]
        r = [rad_ref[rows, C * k : C * (k + 1)] for k in range(4)]
        ud = u[0] * d[1] + u[1] * d[2] + u[2] * d[3]
        r1d = r[1] * d[0]
        dx = [r[0] * d[0] + r[2] * ud] + [r1d * u[k] + r[3] * d[k + 1] for k in range(3)]
        grad_table[...] += hot2(src_hot[:, rows], jnp.concatenate(dx, axis=1), 1, 0)
        return 0

    lax.fori_loop(0, n_chunks, second_scatter, 0)
    send_all(2)

    def second_back(c, _):
        rows = rows_of(c)
        d = spread_rows(c)
        s, v = x_ref[rows, 0:C], [x_ref[rows, C * k : C * (k + 1)] for k in (1, 2, 3)]
        u = [u_ref[rows, LANES * k : LANES * (k + 1)] for k in range(3)]
        uv = u[0] * v[0] + u[1] * v[1] + u[2] * v[2]
        ud = u[0] * d[1] + u[1] * d[2] + u[2] * d[3]
        dv = d[1] * v[0] + d[2] * v[1] + d[3] * v[2]
        drad = jnp.concatenate([d[0] * s, d[0] * uv, s * ud, dv], axis=1)
        hi, lo = split(drad)
        dh = mm(hi, w2_k[0:LANES, :], 1, 1)
        dh = dh + pltpu.roll(dh, hidden, 1) + mm(lo, w2_k[LANES:, :], 1, 1)
        dh_ref[rows, :] = upper_half(dh, 0.0)
        r1d = rad_ref[rows, C : 2 * C] * d[0]
        r2s = rad_ref[rows, 2 * C : 3 * C] * s
        du = lane_sum(0, r1d * v[0] + r2s * d[1])
        for k in (1, 2):
            du = du + lane_sum(k, r1d * v[k] + r2s * d[k + 1])
        du_ref[rows, :] = du
        return 0

    lax.fori_loop(0, n_chunks, second_back, 0)
    wait_all(2)
    ghost_grad = grad_in[0]
    for s in range(1, 9):
        ghost_grad = ghost_grad + grad_in[s]
    dfeat = grad_table[0:atoms, :] + hot3(listed, ghost_grad, 0, 0)
    ds = dfeat[:, 0:C] + ds_direct
    dv = [dfeat[:, C * k : C * (k + 1)] for k in (1, 2, 3)]
    dq = dot3(ds, mq1_ref[...], 1, 0)
    da = ds + 2.0 * a1 * dq + (dv[0] * b1[0] + dv[1] * b1[1] + dv[2] * b1[2])
    db = [dv[k] * (1.0 + a1) + 2.0 * b1[k] * dq for k in range(3)]
    dagg = [dot3(da, ms1_ref[...], 1, 0) * scale]
    db = dot3(jnp.concatenate(db, axis=0), mv1_ref[...], 1, 0) * scale
    dagg += [db[k * atoms : (k + 1) * atoms] for k in range(3)]
    for k in range(4):
        weight = w1[:, 0:C] if k == 0 else w1[:, C : 2 * C]
        spread_grad = jnp.concatenate([dagg[k]] * kinds_n, axis=0) * embed_rows
        hi, lo = split(dot3(spread_grad, weight, 1, 1))
        gp[:, LANES * k : LANES * (k + 1)] = jnp.concatenate([hi, lo], axis=0)

    def first_back(c, _):
        rows = rows_of(c)
        hot = spec_hot[:, rows]
        g = mm(hot, gp[...], 0, 0)
        hid = hid_ref[rows, :]
        dh = dh_ref[rows, :] + g[:, 0:LANES]
        q = du_ref[rows, :]
        for k in range(3):
            gk = g[:, LANES * (k + 1) : LANES * (k + 2)]
            dh = dh + u_ref[rows, LANES * k : LANES * (k + 1)] * gk
            q = q + lane_sum(k, hid * gk)
        dp2 = dh * ds2_ref[rows, :]
        dp1 = dot_k(dp2, wmid_b, 0) * ds1_ref[rows, :]
        q = q + dot_k(dp1, winp_k, 1)
        qt[:, rows] = jnp.transpose(q)
        return 0

    lax.fori_loop(0, n_chunks, first_back, 0)

    unit = v8[...]
    inv = inv_ref[...]
    dr = jnp.sum(qt[0:n_basis, :] * dbas[...], axis=0, keepdims=True)
    du = qt[8:16, :]
    along = jnp.sum(unit * du, axis=0, keepdims=True)
    g8 = dr * unit + (du - unit * along) * inv
    g_hi, g_mid, g_lo = split3(g8)
    hot = src_hot[...]
    force_table[...] = jnp.zeros_like(force_table)
    force_table[:, 0:8] = mm(hot, g_hi, 1, 1) + (mm(hot, g_mid, 1, 1) + mm(hot, g_lo, 1, 1))
    send_all(3)
    own = (live_hot[...] - src_hot[0:atoms, :].astype(f32)).astype(bf16)
    force = mm(g_hi, own, 1, 1) + (mm(g_mid, own, 1, 1) + mm(g_lo, own, 1, 1))
    wait_all(3)
    ghost_force = force_in[0]
    for s in range(1, 9):
        ghost_force = ghost_force + force_in[s]
    hi, mid, lo = split3(ghost_force)
    late = mm(hi, listed, 0, 0) + (mm(mid, listed, 0, 0) + mm(lo, listed, 0, 0))
    force_ref[...] = (force - late[0:8, :])[0:3, :]


def on_device(n_dom, n_sub, *args):
    (vec, senders, counts, species, send_list, embed) = args[:6]
    weights = list(args[6:18])
    read_lin, read_hidden, read_out = args[18:]
    edges = vec.shape[1]
    atoms = species.shape[0]
    ghosts = send_list.shape[0]
    channels, kinds_n = embed.shape
    n_basis = weights[0].shape[1]
    for i in (0, 2, 6, 8):
        weights[i] = weights[i].T
    entries = -(-(atoms + 9 * ghosts) // LANES) * LANES
    wide = 4 * channels
    row = lambda x: x.reshape(1, -1)
    scratch = [
        ((entries, LANES), f32),
        ((ghosts, LANES), f32),
        ((entries, wide), f32),
        ((ghosts, wide), f32),
        ((entries, wide), f32),
        ((9, ghosts, wide), f32),
        ((entries, LANES), f32),
        ((9, ghosts, LANES), f32),
        ((atoms, edges), f32),
        ((2 * kinds_n * atoms, edges), bf16),
        ((entries, edges), bf16),
        ((8, edges), f32),
        ((n_basis, edges), f32),
        ((1, edges), f32),
        ((3 * n_basis + 24, edges), bf16),
        ((3 * n_basis + 24, 4 * LANES), f32),
        ((3 * n_basis + 24, 4 * LANES), bf16),
        ((LANES, LANES), f32),
        ((LANES, 3 * LANES), bf16),
        ((LANES, LANES), f32),
        ((LANES, 3 * LANES), bf16),
        ((3 * LANES, LANES), bf16),
        ((LANES, 2 * channels), f32),
        ((2 * LANES, wide), bf16),
        ((edges, LANES), f32),
        ((edges, 3 * LANES), f32),
        ((edges, LANES), f32),
        ((edges, LANES), f32),
        ((edges, wide), f32),
        ((edges, wide), f32),
        ((kinds_n * atoms, 4 * LANES), f32),
        ((atoms, wide), f32),
        ((atoms, wide), f32),
        ((edges, LANES), f32),
        ((edges, LANES), f32),
        ((2 * kinds_n * atoms, 4 * LANES), bf16),
        ((LANES, edges), f32),
    ]
    whole = pl.BlockSpec(memory_space=pltpu.VMEM)
    energy, force = pl.pallas_call(
        functools.partial(kernel, n_dom, n_sub),
        out_shape=(
            jax.ShapeDtypeStruct((1, atoms), f32),
            jax.ShapeDtypeStruct((3, atoms), f32),
        ),
        in_specs=[whole] * 21,
        out_specs=(whole, whole),
        scratch_shapes=[pltpu.VMEM(shape, dtype) for shape, dtype in scratch]
        + [pltpu.SemaphoreType.DMA((4, 9)), pltpu.SemaphoreType.DMA((4, 9))],
        compiler_params=pltpu.CompilerParams(
            collective_id=0, has_side_effects=True, vmem_limit_bytes=56 * 1024 * 1024
        ),
    )(
        vec,
        row(senders),
        row(counts),
        row(species),
        row(send_list),
        embed.T,
        *weights,
        row(read_lin),
        read_hidden,
        row(read_out),
    )
    return energy.reshape(-1), force


def solution(mesh):
    one = P(("dom", "sub"))
    return jax.shard_map(
        functools.partial(on_device, mesh.shape["dom"], mesh.shape["sub"]),
        mesh=mesh,
        in_specs=(P(None, ("dom", "sub")), one, one, one, one) + (P(),) * 16,
        out_specs=(one, P(None, ("dom", "sub"))),
        check_vma=False,
    )
```

```python
import functools
import math

import jax
import jax.numpy as jnp
from jax import lax
from jax.experimental import pallas as pl
from jax.experimental.pallas import tpu as pltpu
from jax.sharding import PartitionSpec as P

cutoff_radius = 5.0
f32 = jnp.float32
bf16 = jnp.bfloat16
LANES = 128
MESH = pl.DeviceIdType.MESH


def mm(a, b, ca, cb):
    return lax.dot_general(a, b, (((ca,), (cb,)), ((), ())), preferred_element_type=f32)


def split(x):
    hi = x.astype(bf16)
    return hi, (x - hi.astype(f32)).astype(bf16)


def split3(x):
    hi = x.astype(bf16)
    rest = x - hi.astype(f32)
    mid = rest.astype(bf16)
    return hi, mid, (rest - mid.astype(f32)).astype(bf16)


def dot3(a, b, ca, cb):
    a_hi, a_lo = split(a)
    b_hi, b_lo = split(b)
    return mm(a_hi, b_hi, ca, cb) + (mm(a_hi, b_lo, ca, cb) + mm(a_lo, b_hi, ca, cb))


def hot2(hot, x, ca, cb):
    hi, lo = split(x)
    return mm(hot, hi, ca, cb) + mm(hot, lo, ca, cb)


def hot3(hot, x, ca, cb):
    hi, mid, lo = split3(x)
    return mm(hot, hi, ca, cb) + (mm(hot, mid, ca, cb) + mm(hot, lo, ca, cb))


def to_column(row):
    count = row.shape[1]
    shape = (count, count)
    same = lax.broadcasted_iota(jnp.int32, shape, 0) == lax.broadcasted_iota(jnp.int32, shape, 1)
    return jnp.sum(jnp.where(same, row, 0.0), axis=1, keepdims=True)


def series(t, first, terms):
    total = jnp.ones_like(t)
    for i in reversed(range(terms)):
        low = first + 2 * i
        total = 1.0 - t * (1.0 / (low * (low + 1))) * total
    return total


def kernel(
    n_dom,
    n_sub,
    vec_ref,
    senders_ref,
    counts_ref,
    species_ref,
    list_ref,
    embed_ref,
    win1_ref,
    wmid1_ref,
    wout1_ref,
    ms1_ref,
    mv1_ref,
    mq1_ref,
    win2_ref,
    wmid2_ref,
    wout2_ref,
    ms2_ref,
    mv2_ref,
    mq2_ref,
    lin_ref,
    rh_ref,
    ro_ref,
    out_ref,
    kinds,
    kinds_out,
    table,
    feat_out,
    grad_table,
    grad_in,
    force_table,
    force_in,
    live_hot,
    spec_hot,
    src_hot,
    v8,
    dbas,
    inv_ref,
    pack,
    rhs,
    wide_rhs,
    winp,
    winp_k,
    wmid,
    wmid_f,
    wmid_b,
    w1,
    w2_k,
    hid_ref,
    u_ref,
    ds1_ref,
    ds2_ref,
    rad_ref,
    x_ref,
    sums,
    agg2,
    dagg2,
    dh_ref,
    du_ref,
    gp,
    qt,
    send_sem,
    recv_sem,
):
    dm, sb = lax.axis_index("dom"), lax.axis_index("sub")
    atoms = species_ref.shape[1]
    edges = vec_ref.shape[1]
    slots = edges // atoms
    ghosts = list_ref.shape[1]
    kinds_n, channels = embed_ref.shape
    n_basis, hidden = win1_ref.shape
    chunk = 8 * slots
    n_chunks = edges // chunk
    scale = slots ** (-0.5)
    C = channels
    sides = [s for s in range(9) if s != 4]

    def exists(s):
        ok = None
        for here, count, off in ((dm, n_dom, s // 3 - 1), (sb, n_sub, s % 3 - 1)):
            if off == 0:
                continue
            one = here > 0 if off < 0 else here < count - 1
            ok = one if ok is None else jnp.logical_and(ok, one)
        return ok

    def place(s):
        return (dm + (s // 3 - 1), sb + (s % 3 - 1))

    def copy_for(phase, s, src, dst, there):
        return pltpu.make_async_remote_copy(
            src_ref=src,
            dst_ref=dst,
            send_sem=send_sem.at[phase, s],
            recv_sem=recv_sem.at[phase, 8 - s],
            device_id=place(there),
            device_id_type=MESH,
        )

    def ghost_rows(s):
        return pl.ds(atoms + ghosts * s, ghosts)

    def copies(phase, s, there):
        pairs = (
            lambda k, r: (kinds_out, kinds.at[ghost_rows(r)]),
            lambda k, r: (feat_out, table.at[ghost_rows(r)]),
            lambda k, r: (grad_table.at[ghost_rows(k)], grad_in.at[r]),
            lambda k, r: (force_table.at[ghost_rows(k)], force_in.at[r]),
        )
        src, dst = pairs[phase](s, 8 - s)
        return copy_for(phase, s, src, dst, there)

    def send_all(phase):
        for s in sides:
            @pl.when(exists(s))
            def _():
                copies(phase, s, s).start()

    def wait_all(phase):
        for s in sides:
            @pl.when(exists(s))
            def _():
                copies(phase, s, s).wait_send()
                copies(phase, 8 - s, s).wait_recv()

    kinds[...] = jnp.zeros_like(kinds)
    table[...] = jnp.zeros_like(table)
    grad_in[...] = jnp.zeros_like(grad_in)
    force_in[...] = jnp.zeros_like(force_in)
    barrier = pltpu.get_barrier_semaphore()
    for s in sides:
        @pl.when(exists(s))
        def _():
            pl.semaphore_signal(barrier, inc=1, device_id=place(s), device_id_type=MESH)

    species_col = to_column(species_ref[...].astype(f32))
    counts_col = to_column(counts_ref[...].astype(f32)).astype(jnp.int32)
    list_col = to_column(list_ref[...].astype(f32))
    lane_a = lax.broadcasted_iota(jnp.int32, (atoms, LANES), 1).astype(f32)
    own_kinds = (species_col == lane_a).astype(f32)
    kinds[0:atoms, :] = own_kinds
    listed = (
        list_col == lax.broadcasted_iota(jnp.int32, (ghosts, atoms), 1).astype(f32)
    ).astype(f32).astype(bf16)
    kinds_out[...] = mm(listed, own_kinds.astype(bf16), 1, 0)

    wmid[...] = jnp.zeros_like(wmid)
    wmid[0:hidden, 0:hidden] = wmid1_ref[...]
    wmid[hidden:, hidden:] = wmid2_ref[...]
    hi, lo = split(wmid[...])
    wmid_f[...] = jnp.concatenate([hi, hi, lo], axis=1)
    wmid_b[...] = jnp.concatenate([hi, hi, lo], axis=0)
    w1[...] = jnp.zeros_like(w1)
    w1[0:hidden, :] = wout1_ref[...]
    hi, lo = split(wout2_ref[...])
    w2_k[...] = jnp.concatenate([lo, hi, jnp.zeros_like(hi), hi], axis=0)
    winp[...] = jnp.zeros_like(winp)
    winp[0:n_basis, 0:hidden] = win1_ref[...]
    winp[0:n_basis, hidden:] = win2_ref[...]
    hi, lo = split(winp[...])
    winp_k[...] = jnp.concatenate([hi, hi, lo], axis=1)
    n_pack = 3 * n_basis
    row_i = lax.broadcasted_iota(jnp.int32, rhs.shape, 0)
    lane_i = lax.broadcasted_iota(jnp.int32, rhs.shape, 1)
    which = jnp.zeros(rhs.shape, f32)
    for k in range(3):
        in_lanes = (lane_i >= LANES * (k + 1)) & (lane_i < LANES * (k + 2))
        for part in range(3):
            which = jnp.where(in_lanes & (row_i == n_pack + 8 * part + k), 1.0, which)
    rhs[...] = which
    hi, lo = split(winp[0:n_basis, :])
    rhs[0:n_basis, 0:LANES] = hi.astype(f32)
    rhs[n_basis : 2 * n_basis, 0:LANES] = hi.astype(f32)
    rhs[2 * n_basis : 3 * n_basis, 0:LANES] = lo.astype(f32)
    wide_rhs[...] = rhs[...].astype(bf16)

    def dot_k(a, stacked, dim):
        a_hi, a_lo = split(a)
        both = jnp.concatenate([a_hi, a_lo], axis=1)
        if dim == 1:
            first, last = stacked[:, : 2 * LANES], stacked[:, 2 * LANES :]
        else:
            first, last = stacked[: 2 * LANES, :], stacked[2 * LANES :, :]
        return mm(both, first, 1, dim) + mm(a_hi, last, 1, dim)

    def upper_half(x, other):
        lane = lax.broadcasted_iota(jnp.int32, x.shape, 1)
        return jnp.where(lane >= hidden, x, other)

    v8[...] = jnp.zeros_like(v8)
    v8[0:3, :] = vec_ref[...]
    vectors = v8[...]
    dist = jnp.sqrt(jnp.sum(vectors * vectors, axis=0, keepdims=True))
    inv = 1.0 / dist
    unit = vectors * inv
    v8[...] = unit
    inv_ref[...] = inv
    x1 = dist * (1.0 / cutoff_radius)
    x2 = x1 * x1
    x5 = x2 * x2 * x1
    x6 = x5 * x1
    env = 1.0 + x6 * (-28.0 + x1 * (48.0 - 21.0 * x1))
    denv = x5 * (-168.0 + x1 * (336.0 - 168.0 * x1)) * (1.0 / cutoff_radius)
    order = (lax.broadcasted_iota(jnp.int32, (n_basis, edges), 0) + 1).astype(f32)
    turns = order * x1
    near = jnp.floor(turns + 0.5)
    odd = near - 2.0 * jnp.floor(near * 0.5)
    sign = 1.0 - 2.0 * odd
    angle = (turns - near) * math.pi
    t = angle * angle
    sine = sign * angle * series(t, 2, 7)
    cosine = sign * series(t, 1, 7)
    norm = math.sqrt(2.0 / cutoff_radius)
    wave = (norm * inv) * sine
    basis = wave * env
    dbas[...] = ((norm * math.pi / cutoff_radius) * order * cosine * inv - wave * inv) * env + wave * denv

    peers = [
        1 + jnp.where(at > 0, 1, 0) + jnp.where(at < count - 1, 1, 0)
        for at, count in ((dm, n_dom), (sb, n_sub))
    ]
    pl.semaphore_wait(barrier, peers[0] * peers[1] - 1)
    send_all(0)

    b_hi, b_lo = split(basis)
    u_hi, u_mid, u_lo = split3(unit)
    parts = [b_hi, b_lo, b_hi, u_hi, u_mid, u_lo]
    pack[...] = jnp.concatenate([p.astype(f32) for p in parts], axis=0).astype(bf16)

    def rows_of(c):
        return slice(c * chunk, (c + 1) * chunk)

    def each_chunk(step):
        for c in range(n_chunks):
            step(c, 0)

    def radial_step(c, _):
        rows = rows_of(c)
        out = mm(pack[:, rows], wide_rhs[...], 0, 0)
        p1 = out[:, :LANES]
        u_ref[rows, :] = out[:, LANES:]
        s1 = jax.nn.sigmoid(p1)
        h1 = p1 * s1
        ds1_ref[rows, :] = s1 * (1.0 + p1 * (1.0 - s1))
        p2 = dot_k(h1, wmid_f, 1)
        s2 = jax.nn.sigmoid(p2)
        hid_ref[rows, :] = p2 * s2
        ds2_ref[rows, :] = s2 * (1.0 + p2 * (1.0 - s2))
        return 0

    each_chunk(radial_step)

    edge_i = lax.broadcasted_iota(jnp.int32, (atoms, edges), 1)
    atom_i = lax.broadcasted_iota(jnp.int32, (atoms, edges), 0)
    spot = edge_i - atom_i * slots
    live = ((spot >= 0) & (spot < counts_col)).astype(f32)
    live_hot[...] = live
    live_row = jnp.sum(live, axis=0, keepdims=True)
    entry_i = lax.broadcasted_iota(jnp.int32, src_hot.shape, 0)
    src_hot[...] = jnp.where(entry_i == senders_ref[...], live_row, 0.0).astype(bf16)

    own_kinds = kinds[0:atoms, :]
    spread_i = lax.broadcasted_iota(jnp.int32, (kinds_n * atoms, kinds_n), 0)
    kind_i = lax.broadcasted_iota(jnp.int32, (kinds_n * atoms, kinds_n), 1)
    spread = ((spread_i >= kind_i * atoms) & (spread_i < (kind_i + 1) * atoms)).astype(f32).astype(bf16)
    embed_rows = hot3(spread, embed_ref[...], 1, 0)
    initial = hot3(own_kinds[:, 0:kinds_n].astype(bf16), embed_ref[...], 1, 0)

    wait_all(0)
    seen = mm(kinds[...].astype(bf16), src_hot[...], 0, 0)
    for s in range(kinds_n):
        hot = (live_hot[...] * seen[s : s + 1, :]).astype(bf16)
        spec_hot[s * atoms : (s + 1) * atoms, :] = hot
        spec_hot[(kinds_n + s) * atoms : (kinds_n + s + 1) * atoms, :] = hot

    sums[...] = jnp.zeros_like(sums)

    def first_step(c, _):
        rows = rows_of(c)
        hid = hid_ref[rows, :]
        hot = spec_hot[0 : kinds_n * atoms, rows]
        turned = [hid * u_ref[rows, LANES * k : LANES * (k + 1)] for k in range(3)]
        sums[...] += hot2(hot, jnp.concatenate([hid] + turned, axis=1), 1, 0)
        return 0

    each_chunk(first_step)

    def by_kind(x):
        total = x[0:atoms]
        for s in range(1, kinds_n):
            total = total + x[s * atoms : (s + 1) * atoms]
        return total

    agg = []
    for k in range(4):
        weight = w1[:, 0:C] if k == 0 else w1[:, C : 2 * C]
        spread_agg = dot3(sums[:, LANES * k : LANES * (k + 1)], weight, 1, 0)
        agg.append(by_kind(spread_agg * embed_rows) * scale)

    def mixed(parts, ms, mv, mq):
        a = dot3(parts[0], ms, 1, 1)
        b = dot3(jnp.concatenate(parts[1:], axis=0), mv, 1, 1)
        b = [b[k * atoms : (k + 1) * atoms] for k in range(3)]
        squares = a * a + (b[0] * b[0] + b[1] * b[1] + b[2] * b[2])
        return a, b, dot3(squares, mq, 1, 1)

    a1, b1, q1 = mixed(agg, ms1_ref[...], mv1_ref[...], mq1_ref[...])
    scalar_one = initial + a1 + q1
    feats = [scalar_one] + [b + b * a1 for b in b1]
    for k in range(4):
        table[0:atoms, C * k : C * (k + 1)] = feats[k]
        feat_out[:, C * k : C * (k + 1)] = hot3(listed, feats[k], 1, 0)
    send_all(1)

    def second_radial(c, _):
        rows = rows_of(c)
        hid = hid_ref[rows, :]
        twice = upper_half(hid, pltpu.roll(hid, hidden, 1)).astype(bf16)
        rest = split(hid)[1]
        rad_ref[rows, :] = mm(jnp.concatenate([twice, rest], axis=1), w2_k[...], 1, 0)
        return 0

    each_chunk(second_radial)
    wait_all(1)

    def second_step(c, _):
        rows = rows_of(c)
        x = hot2(src_hot[:, rows], table[...], 0, 0)
        x_ref[rows, :] = x
        s, v = x[:, :C], [x[:, C * k : C * (k + 1)] for k in (1, 2, 3)]
        u = [u_ref[rows, LANES * k : LANES * (k + 1)] for k in range(3)]
        r = [rad_ref[rows, C * k : C * (k + 1)] for k in range(4)]
        uv = u[0] * v[0] + u[1] * v[1] + u[2] * v[2]
        rs = r[2] * s
        msgs = [r[0] * s + r[1] * uv] + [rs * u[k] + r[3] * v[k] for k in range(3)]
        group = slice(c * 8, (c + 1) * 8)
        for k in range(4):
            agg2[group, C * k : C * (k + 1)] = jnp.sum(msgs[k].reshape(8, slots, C), axis=1) * scale
        return 0

    each_chunk(second_step)

    parts = [agg2[:, C * k : C * (k + 1)] for k in range(4)]
    a2, b2, q2 = mixed(parts, ms2_ref[...], mv2_ref[...], mq2_ref[...])
    scalar_two = scalar_one + a2 + q2
    z = dot3(scalar_two, rh_ref[...], 1, 1)
    sz = jax.nn.sigmoid(z)
    lin8 = jnp.broadcast_to(lin_ref[...], (8, C))
    ro8 = jnp.broadcast_to(ro_ref[...], (8, ro_ref.shape[1]))
    energy = dot3(lin8, scalar_one, 1, 1) + dot3(ro8, z * sz, 1, 1)
    out_ref[3:4, :] = energy[0:1, :]

    dz = ro_ref[...] * (sz * (1.0 + z * (1.0 - sz)))
    ds_two = dot3(dz, rh_ref[...], 1, 0)
    dq = dot3(ds_two, mq2_ref[...], 1, 0)
    da = ds_two + 2.0 * a2 * dq
    dagg2[:, 0:C] = dot3(da, ms2_ref[...], 1, 0) * scale
    db = dot3(jnp.concatenate([2.0 * b * dq for b in b2], axis=0), mv2_ref[...], 1, 0) * scale
    for k in range(3):
        dagg2[:, C * (k + 1) : C * (k + 2)] = db[k * atoms : (k + 1) * atoms]
    ds_direct = ds_two + lin_ref[...]

    def lane_sum(k, x):
        lane = lax.broadcasted_iota(jnp.int32, x.shape, 1)
        return jnp.where(lane == 8 + k, jnp.sum(x, axis=1, keepdims=True), 0.0)

    grad_table[...] = jnp.zeros_like(grad_table)

    def spread_rows(c):
        group = slice(c * 8, (c + 1) * 8)
        out = []
        for k in range(4):
            small = dagg2[group, C * k : C * (k + 1)]
            out.append(jnp.broadcast_to(small[:, None, :], (8, slots, C)).reshape(chunk, C))
        return out

    def second_scatter(c, _):
        rows = rows_of(c)
        d = spread_rows(c)
        u = [u_ref[rows, LANES * k : LANES * (k + 1)] for k in range(3)]
        r = [rad_ref[rows, C * k : C * (k + 1)] for k in range(4)]
        ud = u[0] * d[1] + u[1] * d[2] + u[2] * d[3]
        r1d = r[1] * d[0]
        dx = [r[0] * d[0] + r[2] * ud] + [r1d * u[k] + r[3] * d[k + 1] for k in range(3)]
        grad_table[...] += hot2(src_hot[:, rows], jnp.concatenate(dx, axis=1), 1, 0)
        return 0

    each_chunk(second_scatter)
    send_all(2)

    def second_back(c, _):
        rows = rows_of(c)
        d = spread_rows(c)
        s, v = x_ref[rows, 0:C], [x_ref[rows, C * k : C * (k + 1)] for k in (1, 2, 3)]
        u = [u_ref[rows, LANES * k : LANES * (k + 1)] for k in range(3)]
        uv = u[0] * v[0] + u[1] * v[1] + u[2] * v[2]
        ud = u[0] * d[1] + u[1] * d[2] + u[2] * d[3]
        dv = d[1] * v[0] + d[2] * v[1] + d[3] * v[2]
        drad = jnp.concatenate([d[0] * s, d[0] * uv, s * ud, dv], axis=1)
        hi, lo = split(drad)
        dh = mm(hi, w2_k[0:LANES, :], 1, 1)
        dh = dh + pltpu.roll(dh, hidden, 1) + mm(lo, w2_k[LANES:, :], 1, 1)
        dh_ref[rows, :] = upper_half(dh, 0.0)
        r1d = rad_ref[rows, C : 2 * C] * d[0]
        r2s = rad_ref[rows, 2 * C : 3 * C] * s
        du = lane_sum(0, r1d * v[0] + r2s * d[1])
        for k in (1, 2):
            du = du + lane_sum(k, r1d * v[k] + r2s * d[k + 1])
        du_ref[rows, :] = du
        return 0

    each_chunk(second_back)
    wait_all(2)
    ghost_grad = grad_in[0]
    for s in range(1, 9):
        ghost_grad = ghost_grad + grad_in[s]
    dfeat = grad_table[0:atoms, :] + hot3(listed, ghost_grad, 0, 0)
    ds = dfeat[:, 0:C] + ds_direct
    dv = [dfeat[:, C * k : C * (k + 1)] for k in (1, 2, 3)]
    dq = dot3(ds, mq1_ref[...], 1, 0)
    da = ds + 2.0 * a1 * dq + (dv[0] * b1[0] + dv[1] * b1[1] + dv[2] * b1[2])
    db = [dv[k] * (1.0 + a1) + 2.0 * b1[k] * dq for k in range(3)]
    dagg = [dot3(da, ms1_ref[...], 1, 0) * scale]
    db = dot3(jnp.concatenate(db, axis=0), mv1_ref[...], 1, 0) * scale
    dagg += [db[k * atoms : (k + 1) * atoms] for k in range(3)]
    for k in range(4):
        weight = w1[:, 0:C] if k == 0 else w1[:, C : 2 * C]
        spread_grad = jnp.concatenate([dagg[k]] * kinds_n, axis=0) * embed_rows
        hi, lo = split(dot3(spread_grad, weight, 1, 1))
        gp[:, LANES * k : LANES * (k + 1)] = jnp.concatenate([hi, lo], axis=0)

    def first_back(c, _):
        rows = rows_of(c)
        hot = spec_hot[:, rows]
        g = mm(hot, gp[...], 0, 0)
        hid = hid_ref[rows, :]
        dh = dh_ref[rows, :] + g[:, 0:LANES]
        q = du_ref[rows, :]
        for k in range(3):
            gk = g[:, LANES * (k + 1) : LANES * (k + 2)]
            dh = dh + u_ref[rows, LANES * k : LANES * (k + 1)] * gk
            q = q + lane_sum(k, hid * gk)
        dp2 = dh * ds2_ref[rows, :]
        dp1 = dot_k(dp2, wmid_b, 0) * ds1_ref[rows, :]
        q = q + dot_k(dp1, winp_k, 1)
        qt[:, rows] = jnp.transpose(q)
        return 0

    each_chunk(first_back)

    unit = v8[...]
    inv = inv_ref[...]
    dr = jnp.sum(qt[0:n_basis, :] * dbas[...], axis=0, keepdims=True)
    du = qt[8:16, :]
    along = jnp.sum(unit * du, axis=0, keepdims=True)
    g8 = dr * unit + (du - unit * along) * inv
    g_hi, g_mid, g_lo = split3(g8)
    hot = src_hot[...]
    force_table[...] = jnp.zeros_like(force_table)
    force_table[:, 0:8] = mm(hot, g_hi, 1, 1) + (mm(hot, g_mid, 1, 1) + mm(hot, g_lo, 1, 1))
    send_all(3)
    own = (live_hot[...] - src_hot[0:atoms, :].astype(f32)).astype(bf16)
    force = mm(g_hi, own, 1, 1) + (mm(g_mid, own, 1, 1) + mm(g_lo, own, 1, 1))
    wait_all(3)
    ghost_force = force_in[0]
    for s in range(1, 9):
        ghost_force = ghost_force + force_in[s]
    hi, mid, lo = split3(ghost_force)
    late = mm(hi, listed, 0, 0) + (mm(mid, listed, 0, 0) + mm(lo, listed, 0, 0))
    out_ref[0:3, :] = (force - late[0:8, :])[0:3, :]


def on_device(n_dom, n_sub, *args):
    (vec, senders, counts, species, send_list, embed) = args[:6]
    weights = list(args[6:18])
    read_lin, read_hidden, read_out = args[18:]
    edges = vec.shape[1]
    atoms = species.shape[0]
    ghosts = send_list.shape[0]
    channels, kinds_n = embed.shape
    n_basis = weights[0].shape[1]
    for i in (0, 2, 6, 8):
        weights[i] = weights[i].T
    entries = -(-(atoms + 9 * ghosts) // LANES) * LANES
    wide = 4 * channels
    row = lambda x: x.reshape(1, -1)
    scratch = [
        ((entries, LANES), f32),
        ((ghosts, LANES), f32),
        ((entries, wide), f32),
        ((ghosts, wide), f32),
        ((entries, wide), f32),
        ((9, ghosts, wide), f32),
        ((entries, LANES), f32),
        ((9, ghosts, LANES), f32),
        ((atoms, edges), f32),
        ((2 * kinds_n * atoms, edges), bf16),
        ((entries, edges), bf16),
        ((8, edges), f32),
        ((n_basis, edges), f32),
        ((1, edges), f32),
        ((3 * n_basis + 24, edges), bf16),
        ((3 * n_basis + 24, 4 * LANES), f32),
        ((3 * n_basis + 24, 4 * LANES), bf16),
        ((LANES, LANES), f32),
        ((LANES, 3 * LANES), bf16),
        ((LANES, LANES), f32),
        ((LANES, 3 * LANES), bf16),
        ((3 * LANES, LANES), bf16),
        ((LANES, 2 * channels), f32),
        ((2 * LANES, wide), bf16),
        ((edges, LANES), f32),
        ((edges, 3 * LANES), f32),
        ((edges, LANES), f32),
        ((edges, LANES), f32),
        ((edges, wide), f32),
        ((edges, wide), f32),
        ((kinds_n * atoms, 4 * LANES), f32),
        ((atoms, wide), f32),
        ((atoms, wide), f32),
        ((edges, LANES), f32),
        ((edges, LANES), f32),
        ((2 * kinds_n * atoms, 4 * LANES), bf16),
        ((LANES, edges), f32),
    ]
    whole = pl.BlockSpec(memory_space=pltpu.VMEM)
    out = pl.pallas_call(
        functools.partial(kernel, n_dom, n_sub),
        out_shape=jax.ShapeDtypeStruct((4, atoms), f32),
        in_specs=[whole] * 21,
        out_specs=whole,
        scratch_shapes=[pltpu.VMEM(shape, dtype) for shape, dtype in scratch]
        + [pltpu.SemaphoreType.DMA((4, 9)), pltpu.SemaphoreType.DMA((4, 9))],
        compiler_params=pltpu.CompilerParams(
            collective_id=0, has_side_effects=True, vmem_limit_bytes=56 * 1024 * 1024
        ),
    )(
        vec,
        row(senders),
        row(counts),
        row(species),
        row(send_list),
        embed.T,
        *weights,
        row(read_lin),
        read_hidden,
        row(read_out),
    )
    return out[3], out[0:3]


def solution(mesh):
    one = P(("dom", "sub"))
    return jax.shard_map(
        functools.partial(on_device, mesh.shape["dom"], mesh.shape["sub"]),
        mesh=mesh,
        in_specs=(P(None, ("dom", "sub")), one, one, one, one) + (P(),) * 16,
        out_specs=(one, P(None, ("dom", "sub"))),
        check_vma=False,
    )
```
